256 devices in a mesh: wide: 64 (over z_lo, x, y), narrow: 4 (over z_hi, core).
Axes of the slice: x: 4, y: 4, z: 8 (z_hi: 2, z_lo: 4; z = z_hi * 4 + z_lo), core: 2. Of those that a mesh axis runs over, the one named last changes fastest.
Arguments:
- constraint_mats: bfloat16 [1024, 256, 256], P(('narrow', 'wide')), may hold values from -0.375 to 0.375
- primal_matrix: bfloat16 [256, 256], replicated, may hold values from -0.25 to 0.25
- inverse_dual_iterate: bfloat16 [256, 256], replicated, may hold values from -0.25 to 0.25
Outputs:
- schur: float32 [1024, 1024], P(('narrow', 'wide'))
The draws below stay inside these ranges and needn't reach their ends.
All inputs are finite; a program needn't handle non-finite values.
Results may differ from the reference program's by a relative error of at most 0.0029.
Values may be sent and summed in bfloat16 or wider, within the bound.
A program may use at most 64 MiB of HBM per device.

```python
import jax
import jax.numpy as jnp

ORDER = 256
M_TOT = 1024


def symmetric_draw(key, shape, scale, limit):
    raw = jnp.clip(jax.random.normal(key, shape, jnp.float32) * scale, -limit, limit)
    return 0.5 * (raw + jnp.swapaxes(raw, -1, -2))


def draw_constraint_mats(key, part):
    return symmetric_draw(key, (M_TOT, ORDER, ORDER), 0.0625, 0.375).astype(jnp.bfloat16)


def draw_primal_matrix(key, part):
    return symmetric_draw(jax.random.fold_in(key, 11), (ORDER, ORDER), 0.0625, 0.25).astype(jnp.bfloat16)


def draw_inverse_dual_iterate(key, part):
    return symmetric_draw(jax.random.fold_in(key, 23), (ORDER, ORDER), 0.0625, 0.25).astype(jnp.bfloat16)


def setup_inputs(seed: int = 0) -> dict:
    keys = jax.random.split(jax.random.key(seed), 4)
    constraint_mats = draw_constraint_mats(jax.random.fold_in(keys[3], 71), 0)
    primal_matrix = draw_primal_matrix(jax.random.fold_in(keys[3], 71), 0)
    inverse_dual_iterate = draw_inverse_dual_iterate(jax.random.fold_in(keys[3], 71), 0)
    return {"constraint_mats": constraint_mats, "primal_matrix": primal_matrix, "inverse_dual_iterate": inverse_dual_iterate}


def reference(constraint_mats, primal_matrix, inverse_dual_iterate):
    mats = constraint_mats.astype(jnp.float32)
    left_product = jnp.einsum('ab,ibc->iac', primal_matrix.astype(jnp.float32), mats).astype(jnp.bfloat16)
    product_matrices = jnp.einsum('lsx,xm->lsm', left_product.astype(jnp.float32), inverse_dual_iterate.astype(jnp.float32)).astype(jnp.bfloat16)
    count = constraint_mats.shape[0]
    u_flat = product_matrices.reshape(count, -1).astype(jnp.float32)
    a_flat = mats.reshape(count, -1)
    pairing = jnp.dot(u_flat, a_flat.T)
    return 0.5 * (pairing + pairing.T)
```

```python
import jax
import jax.numpy as jnp
from jax import lax
from jax.sharding import PartitionSpec as P


def contract(u_rows, constraint_row_stack):
    return lax.dot_general(
        u_rows, constraint_row_stack, (((1,), (1,)), ((), ())), preferred_element_type=jnp.float32
    )


def body(constraint_mats, primal_matrix, inverse_dual_iterate):
    count = constraint_mats.shape[0]
    order = constraint_mats.shape[1]
    wide = lax.axis_size("wide")
    left_product = jnp.einsum(
        "ab,ibc->iac", primal_matrix, constraint_mats, preferred_element_type=jnp.float32
    ).astype(jnp.bfloat16)
    product_matrices = jnp.einsum(
        "lsx,xm->lsm", left_product, inverse_dual_iterate, preferred_element_type=jnp.float32
    ).astype(jnp.bfloat16)
    u_flat = product_matrices.reshape(count, order * order)
    a_flat = constraint_mats.reshape(count, order * order)
    both = jnp.stack([u_flat, a_flat])
    pieces = lax.all_to_all(both, "wide", split_axis=2, concat_axis=1, tiled=True)
    every = lax.all_gather(pieces, "narrow", axis=1, tiled=True)
    partial_value = 0.5 * (contract(pieces[0], every[1]) + contract(pieces[1], every[0]))
    rows = partial_value.shape[0] // wide
    blocks = partial_value.reshape(wide, rows, partial_value.shape[1])
    arrived = lax.all_to_all(blocks, "wide", split_axis=0, concat_axis=0, tiled=True)
    return jnp.sum(arrived, axis=0)


def solution(mesh):
    in_specs = (P(("narrow", "wide"), None, None), P(), P())
    out_specs = P(("narrow", "wide"), None)
    return jax.shard_map(body, mesh=mesh, in_specs=in_specs, out_specs=out_specs, check_vma=False)
```
